32 devices in a mesh: grp: 2 (over y), orb: 8 (over z, x), aux: 2 (over core).
Axes of the slice: x: 2, y: 2, z: 4, core: 2. Of those that a mesh axis runs over, the one named last changes fastest.
Arguments:
- half: bfloat16 [8, 8192, 768], P('aux', ('grp', 'orb')), parts along dimension 1, may hold values from -1.75 to 1.75
- pair_mask: int32 [16, 4], P(('grp', 'orb')), parts along dimension 0, may hold values from 0 to 1, as said below
Outputs:
- kband: float32 [8192, 2048], P(('grp', 'orb'), 'aux'), parts along dimension 0
The draws below stay inside these ranges and needn't reach their ends.
There are 2 independent parts, one for each index of `grp`. The reference program is written for one: setup_inputs(seed, part) draws one part's arguments, and reference() takes and returns one part's arrays. A program takes and returns all parts, laid end to end along the dimension named above; each array names one. Nothing has to cross between parts.
Inputs may be any that keep to these rules, and one draw needn't show every extreme that they name: pair_mask[b, 0] is 1 for every block; entries with b + d >= 8 are 0; some block row has all 4 entries 1.
All inputs are finite; a program needn't handle non-finite values.
Results may differ from the reference program's by a relative error of at most 0.0003.
Values may be sent and summed in bfloat16 or wider, within the bound.
A program may use at most 64 MiB of HBM per device.

```python
import jax
import jax.numpy as jnp

BLK = 512
NOCC = 768
NAUXB = 8
NBLK = 8
NBASIS = 4096
WIN = 4


def draw_pair_mask(key, part):
    key_a, key_b, key_c = jax.random.split(jax.random.fold_in(key, 7), 3)
    thresh = jax.random.randint(key_a, (NBLK, 1), 1, WIN + 1)
    coins = jax.random.randint(key_b, (NBLK, WIN), 0, WIN)
    offsets = jnp.arange(WIN)[None, :]
    rows = jnp.arange(NBLK)[:, None]
    full_row = jax.random.randint(key_c, (), 0, NBLK - WIN + 1)
    keep = (coins < thresh) | (offsets == 0) | (rows == full_row)
    valid = rows + offsets < NBLK
    return (keep & valid).astype(jnp.int32)


def steps_of(rng, extent, shards, least, top_value):
    level, own = 1.0, jax.random.fold_in(rng, 6)
    for position, parts in shards:
        steps = jnp.exp(jax.random.uniform(jax.random.fold_in(own, position), (parts,), jnp.float32, least / len(shards), top_value / len(shards)))
        level = level * jnp.repeat(steps, extent[position] // parts).reshape([-1 if axis == position else 1 for axis in range(len(extent))])
    return level


def scatter_about(key, extent, width, most, cuts=(), held_as=jnp.bfloat16):
    drawn = width * jax.random.normal(key, extent, jnp.float32)
    if cuts:
        drawn = drawn * steps_of(key, extent, cuts, -0.22, 0.18)
    return jnp.clip(drawn, -most, most).astype(held_as)


def setup_inputs(seed: int = 0, part: int = 0) -> dict:
    key_list = jax.random.split(jax.random.key(seed), 3)
    part_splits = jax.random.split(jax.random.fold_in(key_list[2], part), 3)
    half = scatter_about(part_splits[0], (NAUXB, NBASIS, NOCC), ((NAUXB * NOCC) ** -0.25), 1.75, ((0, 2), (1, 8)))
    pair_mask = draw_pair_mask(jax.random.fold_in(jax.random.fold_in(key_list[2], part), 71), part)
    return {"half": half, "pair_mask": pair_mask}


def reference(half, pair_mask):
    blocks = half.reshape(NAUXB, NBLK, BLK, NOCC).astype(jnp.float32)
    pieces = []
    for offset in range(WIN):
        remote = jnp.concatenate([blocks[:, offset:], jnp.zeros((NAUXB, offset, BLK, NOCC), jnp.float32)], axis=1)
        tile = jnp.einsum("pbmk,pbnk->bmn", blocks, remote)
        pieces.append(tile * pair_mask[:, offset].astype(jnp.float32)[:, None, None])
    return jnp.concatenate(pieces, axis=2).reshape(NBASIS, WIN * BLK)
```

```python
import functools

import jax
import jax.numpy as jnp
from jax import lax
from jax.experimental import pallas as pl
from jax.experimental.pallas import tpu as pltpu
from jax.sharding import PartitionSpec as P

MESH = pl.DeviceIdType.MESH
CHUNKS = 4
DIAG, INNER, UPPER = 0, 1, 6


def dot_nt(left, right):
    return lax.dot_general(left, right, (((1,), (1,)), ((), ())), preferred_element_type=jnp.float32)


def kernel(
    devices, half_ref, out_ref, pair, rest, above, below, part, sib, landed,
    load_sem, x_send, x_recv, down_send, down_recv, up_send, up_recv,
    sib_send, sib_recv, fwd_send, land_recv,
):
    pairs = devices // 2
    me = lax.axis_index("orb")
    aux = lax.axis_index("aux")
    p, par = lax.div(me, 2), lax.rem(me, 2)
    has_down, has_up, two_up = p > 0, p < pairs - 1, p < pairs - 2
    neighbour = {"orb": me + 1 - 2 * par}
    lower, upper, sibling = {"orb": me - 2}, {"orb": me + 2}, {"aux": 1 - aux}
    lower_odd = {"orb": me - 1 - par}
    depth = pair.shape[1]
    rows = pair.shape[2]
    width = rows // CHUNKS
    mine, other = depth * par, depth * (1 - par)

    def span(c):
        return pl.ds(pl.multiple_of(c * width, width), width)

    def remote(src, dst, send, recv, device):
        return pltpu.make_async_remote_copy(
            src_ref=src, dst_ref=dst, send_sem=send, recv_sem=recv, device_id=device, device_id_type=MESH
        )

    def x_copy(c):
        return remote(half_ref.at[pl.ds(other, depth), span(c), :], pair.at[par, :, span(c), :], x_send.at[c], x_recv.at[c], neighbour)

    def x_arrival(c):
        spot = pair.at[1 - par, :, span(c), :]
        return remote(spot, spot, x_send.at[c], x_recv.at[c], neighbour)

    def down_own(c):
        return remote(half_ref.at[pl.ds(mine, depth), span(c), :], above.at[par, :, span(c), :], down_send.at[0, c], down_recv.at[0, c], lower)

    def down_relay(c):
        return remote(pair.at[1 - par, :, span(c), :], above.at[1 - par, :, span(c), :], down_send.at[1, c], down_recv.at[1, c], lower)

    def down_arrival(phase, q, c):
        spot = above.at[q, :, span(c), :]
        return remote(spot, spot, down_send.at[phase, c], down_recv.at[phase, c], lower)

    def up_own(c):
        return remote(half_ref.at[pl.ds(mine, depth), span(c), :], below.at[:, span(c), :], up_send.at[c], up_recv.at[c], upper)

    def up_relay(c):
        return remote(pair.at[1, :, span(c), :], below.at[:, span(c), :], up_send.at[c], up_recv.at[c], upper)

    def sib_copy(s, c):
        return remote(part.at[s, c], sib.at[s, c], sib_send.at[s, c], sib_recv.at[s, c], sibling)

    def forward(s, c, slot, device):
        return remote(part.at[s, c], landed.at[slot, c], fwd_send.at[s, c], land_recv.at[slot, c], device)

    def each(body):
        def step(c, carry):
            body(c)
            return carry
        lax.fori_loop(0, CHUNKS, step, 0)

    barrier = pltpu.get_barrier_semaphore()

    def greet(device):
        pl.semaphore_signal(barrier, inc=1, device_id=device, device_id_type=MESH)

    greet(neighbour)
    greet(sibling)
    pl.when(has_down)(lambda: greet(lower))
    pl.when(has_up)(lambda: greet(upper))
    pl.when(has_down & (par == 0))(lambda: greet({"orb": me - 1}))
    pl.when(has_up & (par == 1))(lambda: greet({"orb": me + 1}))
    peers_down, peers_up = jnp.where(has_down, 1, 0), jnp.where(has_up, 1, 0)
    pl.semaphore_wait(barrier, 2 + peers_down * (2 - par) + peers_up * (1 + par))

    def launch(c):
        x_copy(c).start()
        pl.when(has_down)(lambda: down_own(c).start())
        pl.when(two_up & (par == 1))(lambda: up_own(c).start())

    each(launch)
    load_mine = pltpu.make_async_copy(half_ref.at[pl.ds(mine, depth)], pair.at[par], load_sem.at[0])
    load_rest = pltpu.make_async_copy(half_ref.at[pl.ds(other, depth)], rest, load_sem.at[1])
    load_mine.start()
    load_rest.start()
    load_mine.wait()
    load_rest.wait()

    def diagonal(c):
        total = dot_nt(pair[par, 0], pair[par, 0, span(c), :])
        for i in range(1, depth):
            total += dot_nt(pair[par, i], pair[par, i, span(c), :])
        for i in range(depth):
            total += dot_nt(rest[i], rest[i, span(c), :])
        part[DIAG, c] = total
        pl.when(aux == 1)(lambda: sib_copy(DIAG, c).start())

    each(diagonal)

    def relay(c):
        x_arrival(c).wait_recv()
        pl.when(has_down)(lambda: down_relay(c).start())
        pl.when(two_up & (par == 0))(lambda: up_relay(c).start())

    each(relay)

    def product(left, right, c):
        total = dot_nt(left[0], right[0, span(c), :])
        for i in range(1, depth):
            total += dot_nt(left[i], right[i, span(c), :])
        return total

    def inner(c):
        part[INNER, c] = product(pair.at[0], pair.at[1], c)

        @pl.when(aux == 1)
        def _():
            sib_copy(INNER, c).start()

    each(inner)

    def inner_sum(c):
        @pl.when((aux == 0) & (par == 1))
        def _():
            sib_copy(INNER, c).wait_recv()
            part[INNER, c] += sib[INNER, c]
            forward(INNER, c, 0, neighbour).start()

    each(inner_sum)

    def below_arrived(c):
        spot = below.at[:, span(c), :]
        remote(spot, spot, up_send.at[c], up_recv.at[c], upper).wait_recv()

    @pl.when(has_up)
    def _():
        def step(t, carry):
            phase, c = lax.div(t, CHUNKS), lax.rem(t, CHUNKS)
            q = par + phase - 2 * par * phase
            own, far = 2 + 2 * phase, 3 + 2 * phase
            own_holder = 1 - par * phase
            far_holder = par + phase - par * phase
            upper_tile = (q == 0) & has_down
            down_arrival(phase, q, c).wait_recv()
            part[far, c] = product(pair.at[1 - par], above.at[q], c)
            pl.when(aux != far_holder)(lambda: sib_copy(far, c).start())

            pl.when(upper_tile & (c == 0))(lambda: each(below_arrived))

            @pl.when(upper_tile)
            def _():
                part[UPPER, c] = product(below, above.at[q], c)
                pl.when(aux == 0)(lambda: sib_copy(UPPER, c).start())

            part[own, c] = product(pair.at[par], above.at[q], c)
            pl.when(aux != own_holder)(lambda: sib_copy(own, c).start())

            @pl.when(aux == far_holder)
            def _():
                sib_copy(far, c).wait_recv()
                part[far, c] += sib[far, c]
                forward(far, c, phase, neighbour).start()

            @pl.when(upper_tile & (aux == 1))
            def _():
                sib_copy(UPPER, c).wait_recv()
                part[UPPER, c] += sib[UPPER, c]
                forward(UPPER, c, 2 * par, lower_odd).start()

            return carry

        lax.fori_loop(0, 2 * CHUNKS, step, 0)

    def columns(k, c):
        return pl.ds(pl.multiple_of(k * rows + c * width, width), width)

    def landing(slot, c):
        spot = landed.at[slot, c]
        return remote(spot, spot, fwd_send.at[0, c], land_recv.at[slot, c], neighbour)

    def finish(k, s, slot):
        def body(c):
            sib_copy(s, c).wait_recv()
            total = part[s, c] + sib[s, c]
            if slot is not None:
                landing(slot, c).wait_recv()
                total += landed[slot, c]
            out_ref[:, columns(k, c)] = total
        each(body)

    def blank(k):
        def body(c):
            out_ref[:, columns(k, c)] = jnp.zeros((rows, width), jnp.float32)
        each(body)

    no_up = jnp.logical_not(has_up)

    @pl.when(aux == 0)
    def _():
        finish(0, DIAG, None)
        pl.when(par == 0)(lambda: finish(1, INNER, 0))
        pl.when((par == 1) & has_up)(lambda: finish(1, 4, 0))
        pl.when((par == 1) & no_up)(lambda: blank(1))

    @pl.when(aux == 1)
    def _():
        pl.when(has_up)(lambda: finish(0, 2, 1))
        pl.when(no_up)(lambda: blank(0))
        pl.when((par == 0) & has_up)(lambda: finish(1, 4, 0))
        pl.when((par == 0) & no_up)(lambda: blank(1))

        @pl.when((par == 1) & two_up)
        def _():
            def body(c):
                landing(0, c).wait_recv()
                landing(2, c).wait_recv()
                out_ref[:, columns(1, c)] = landed[0, c] + landed[2, c]
            each(body)

        pl.when((par == 1) & jnp.logical_not(two_up))(lambda: blank(1))

    def drain(c):
        x_copy(c).wait_send()

        @pl.when(has_down)
        def _():
            down_own(c).wait_send()
            down_relay(c).wait_send()

        pl.when(two_up)(lambda: up_relay(c).wait_send())

        @pl.when(aux == 1)
        def _():
            sib_copy(DIAG, c).wait_send()
            sib_copy(INNER, c).wait_send()

        pl.when((aux == 0) & (par == 1))(lambda: forward(INNER, c, 0, neighbour).wait_send())

        @pl.when(has_up)
        def _():
            for phase in (0, 1):
                own, far = 2 + 2 * phase, 3 + 2 * phase
                own_holder = 1 - par * phase
                far_holder = par + phase - par * phase
                pl.when(aux != own_holder)(lambda: sib_copy(own, c).wait_send())
                pl.when(aux != far_holder)(lambda: sib_copy(far, c).wait_send())
                pl.when(aux == far_holder)(lambda: forward(far, c, phase, neighbour).wait_send())

            @pl.when(has_down)
            def _():
                pl.when(aux == 0)(lambda: sib_copy(UPPER, c).wait_send())
                pl.when(aux == 1)(lambda: forward(UPPER, c, 2 * par, lower_odd).wait_send())

    each(drain)


def per_device(half, pair_mask):
    devices = lax.axis_size("orb")
    aux_count, blk, occ = half.shape
    depth, wide = aux_count // 2, blk // CHUNKS
    f32, bf16 = jnp.float32, jnp.bfloat16
    dma = pltpu.SemaphoreType.DMA
    tiles = pl.pallas_call(
        functools.partial(kernel, devices),
        out_shape=jax.ShapeDtypeStruct((blk, 2 * blk), f32),
        in_specs=[pl.BlockSpec(memory_space=pl.ANY)],
        out_specs=pl.BlockSpec(memory_space=pltpu.VMEM),
        scratch_shapes=[
            pltpu.VMEM((2, depth, blk, occ), bf16),
            pltpu.VMEM((depth, blk, occ), bf16),
            pltpu.VMEM((2, depth, blk, occ), bf16),
            pltpu.VMEM((depth, blk, occ), bf16),
            pltpu.VMEM((7, CHUNKS, blk, wide), f32),
            pltpu.VMEM((7, CHUNKS, blk, wide), f32),
            pltpu.VMEM((3, CHUNKS, blk, wide), f32),
            dma((2,)),
            dma((CHUNKS,)), dma((CHUNKS,)),
            dma((2, CHUNKS)), dma((2, CHUNKS)),
            dma((CHUNKS,)), dma((CHUNKS,)),
            dma((7, CHUNKS)), dma((7, CHUNKS)),
            dma((7, CHUNKS)), dma((3, CHUNKS)),
        ],
        compiler_params=pltpu.CompilerParams(
            collective_id=0, has_side_effects=True, vmem_limit_bytes=48 * 1024 * 1024
        ),
    )(half)
    first = lax.axis_index("aux") * 2
    weight = lax.dynamic_slice(pair_mask, (0, first), (1, 2)).astype(f32)
    return tiles * jnp.repeat(weight, blk, axis=1)


def solution(mesh):
    in_specs = (P("aux", ("grp", "orb"), None), P(("grp", "orb"), None))
    out_specs = P(("grp", "orb"), "aux")
    return jax.shard_map(
        per_device, mesh=mesh, in_specs=in_specs, out_specs=out_specs, check_vma=False
    )
```

```python
import functools

import jax
import jax.numpy as jnp
from jax import lax
from jax.experimental import pallas as pl
from jax.experimental.pallas import tpu as pltpu
from jax.sharding import PartitionSpec as P

MESH = pl.DeviceIdType.MESH
CHUNKS = 4
EARLY = 2
SPLIT = CHUNKS // 2
DIAG, INNER, UPPER = 0, 1, 6


def dot_nt(left, right):
    return lax.dot_general(left, right, (((1,), (1,)), ((), ())), preferred_element_type=jnp.float32)


def kernel(
    devices, half_ref, mask_ref, out_ref, pair, rest, above, below, part, sib, landed,
    load_sem, x_send, x_recv, down_send, down_recv, up_send, up_recv,
    sib_send, sib_recv, fwd_send, land_recv,
):
    pairs = devices // 2
    me = lax.axis_index("orb")
    aux = lax.axis_index("aux")
    p, par = lax.div(me, 2), lax.rem(me, 2)
    has_down, has_up, two_up = p > 0, p < pairs - 1, p < pairs - 2
    neighbour = {"orb": me + 1 - 2 * par}
    lower, upper, sibling = {"orb": me - 2}, {"orb": me + 2}, {"aux": 1 - aux}
    lower_odd = {"orb": me - 1 - par}
    depth = pair.shape[1]
    rows = pair.shape[2]
    width = rows // CHUNKS
    mine, other = depth * par, depth * (1 - par)

    def span(c):
        return pl.ds(pl.multiple_of(c * width, width), width)

    def remote(src, dst, send, recv, device):
        return pltpu.make_async_remote_copy(
            src_ref=src, dst_ref=dst, send_sem=send, recv_sem=recv, device_id=device, device_id_type=MESH
        )

    def x_copy(c):
        return remote(half_ref.at[pl.ds(other, depth), span(c), :], pair.at[par, :, span(c), :], x_send.at[c], x_recv.at[c], neighbour)

    def x_arrival(c):
        spot = pair.at[1 - par, :, span(c), :]
        return remote(spot, spot, x_send.at[c], x_recv.at[c], neighbour)

    def down_own(c):
        return remote(half_ref.at[pl.ds(mine, depth), span(c), :], above.at[par, :, span(c), :], down_send.at[0, c], down_recv.at[0, c], lower)

    def down_relay(c):
        return remote(pair.at[1 - par, :, span(c), :], above.at[1 - par, :, span(c), :], down_send.at[1, c], down_recv.at[1, c], lower)

    def down_arrival(phase, q, c):
        spot = above.at[q, :, span(c), :]
        return remote(spot, spot, down_send.at[phase, c], down_recv.at[phase, c], lower)

    def up_own(c):
        return remote(half_ref.at[pl.ds(mine, depth), span(c), :], below.at[:, span(c), :], up_send.at[c], up_recv.at[c], upper)

    def up_relay(c):
        return remote(pair.at[1, :, span(c), :], below.at[:, span(c), :], up_send.at[c], up_recv.at[c], upper)

    def sib_copy(s, c):
        return remote(part.at[s, c], sib.at[s, c], sib_send.at[s, c], sib_recv.at[s, c], sibling)

    def forward(s, c, slot, device):
        return remote(part.at[s, c], landed.at[slot, c], fwd_send.at[s, c], land_recv.at[slot, c], device)

    def each(body):
        def step(c, carry):
            body(c)
            return carry
        lax.fori_loop(0, CHUNKS, step, 0)

    barrier = pltpu.get_barrier_semaphore()

    def greet(device):
        pl.semaphore_signal(barrier, inc=1, device_id=device, device_id_type=MESH)

    greet(neighbour)
    greet(sibling)
    pl.when(has_down)(lambda: greet(lower))
    pl.when(has_up)(lambda: greet(upper))
    pl.when(has_down & (par == 0))(lambda: greet({"orb": me - 1}))
    pl.when(has_up & (par == 1))(lambda: greet({"orb": me + 1}))
    peers_down, peers_up = jnp.where(has_down, 1, 0), jnp.where(has_up, 1, 0)
    pl.semaphore_wait(barrier, 2 + peers_down * (2 - par) + peers_up * (1 + par))

    early = CHUNKS - par * (CHUNKS - EARLY)

    def launch(c):
        x_copy(c).start()
        pl.when(has_down & (c < early))(lambda: down_own(c).start())
        pl.when(two_up & (par == 1))(lambda: up_own(c).start())

    each(launch)
    load_mine = pltpu.make_async_copy(half_ref.at[pl.ds(mine, depth)], pair.at[par], load_sem.at[0])
    load_rest = pltpu.make_async_copy(half_ref.at[pl.ds(other, depth)], rest, load_sem.at[1])
    load_mine.start()
    load_rest.start()
    load_mine.wait()
    load_rest.wait()

    def diagonal(c):
        total = dot_nt(pair[par, 0], pair[par, 0, span(c), :])
        for i in range(1, depth):
            total += dot_nt(pair[par, i], pair[par, i, span(c), :])
        for i in range(depth):
            total += dot_nt(rest[i], rest[i, span(c), :])
        part[DIAG, c] = total
        pl.when(aux == 1)(lambda: sib_copy(DIAG, c).start())

    each(diagonal)

    def relay(c):
        x_arrival(c).wait_recv()
        pl.when(has_down)(lambda: down_relay(c).start())
        pl.when(two_up & (par == 0))(lambda: up_relay(c).start())

    each(relay)

    @pl.when(has_down & (par == 1))
    def _():
        for c in range(EARLY, CHUNKS):
            down_own(c).start()

    def diagonal_sum(c):
        sib_copy(DIAG, c).wait_recv()
        part[DIAG, c] += sib[DIAG, c]


    def product(left, right, c):
        total = dot_nt(left[0], right[0, span(c), :])
        for i in range(1, depth):
            total += dot_nt(left[i], right[i, span(c), :])
        return total

    def inner(c):
        part[INNER, c] = product(pair.at[0], pair.at[1], c)

        @pl.when(aux == 1)
        def _():
            sib_copy(INNER, c).start()

    each(inner)

    def inner_sum(c):
        sib_copy(INNER, c).wait_recv()
        part[INNER, c] += sib[INNER, c]
        pl.when(par == 1)(lambda: forward(INNER, c, 0, neighbour).start())

    @pl.when(aux == 0)
    def _():
        each(inner_sum)
        each(diagonal_sum)

    def landing(slot, c):
        spot = landed.at[slot, c]
        return remote(spot, spot, fwd_send.at[0, c], land_recv.at[slot, c], neighbour)

    def below_arrived(c):
        spot = below.at[:, span(c), :]
        remote(spot, spot, up_send.at[c], up_recv.at[c], upper).wait_recv()

    @pl.when(has_up)
    def _():
        def step(t, carry):
            middle = (t >= EARLY) & (t < EARLY + CHUNKS)
            q = jnp.where(par == 0, lax.div(t, CHUNKS), jnp.where(middle, 0, 1))
            c = jnp.where(par == 0, lax.rem(t, CHUNKS), jnp.where(middle, t - EARLY, jnp.where(t < EARLY, t, t - CHUNKS)))
            phase = par + q - 2 * par * q
            own, far = 2 + 2 * phase, 3 + 2 * phase
            own_holder = 1 - par * phase
            far_holder = par + phase - par * phase
            upper_tile = (q == 0) & has_down
            down_arrival(phase, q, c).wait_recv()
            part[far, c] = product(pair.at[1 - par], above.at[q], c)
            pl.when(aux != far_holder)(lambda: sib_copy(far, c).start())

            pl.when(upper_tile & (c == 0))(lambda: each(below_arrived))

            @pl.when(upper_tile)
            def _():
                part[UPPER, c] = product(below, above.at[q], c)
                pl.when(aux == 0)(lambda: sib_copy(UPPER, c).start())

            part[own, c] = product(pair.at[par], above.at[q], c)
            pl.when(aux != own_holder)(lambda: sib_copy(own, c).start())

            @pl.when(aux == far_holder)
            def _():
                sib_copy(far, c).wait_recv()
                part[far, c] += sib[far, c]
                forward(far, c, phase, neighbour).start()

            @pl.when(upper_tile & (aux == 1))
            def _():
                sib_copy(UPPER, c).wait_recv()
                part[UPPER, c] += sib[UPPER, c]
                pl.when(lax.div(c, SPLIT) != par)(lambda: forward(UPPER, c, 2, neighbour).start())

            @pl.when((t == EARLY + CHUNKS - 1) & has_down & (aux == 1))
            def _():
                for i in range(SPLIT):
                    k = par * SPLIT + i
                    landing(2, k).wait_recv()
                    part[UPPER, k] += landed[2, k]
                    forward(UPPER, k, 0, lower_odd).start()

            @pl.when(aux == own_holder)
            def _():
                sib_copy(own, c).wait_recv()
                part[own, c] += sib[own, c]

            return carry

        lax.fori_loop(0, 2 * CHUNKS, step, 0)

    def columns(k, c):
        return pl.ds(pl.multiple_of(k * rows + c * width, width), width)

    def finish(k, s, slot):
        weight = mask_ref[0, 2 * aux + k].astype(jnp.float32)

        def body(c):
            total = part[s, c]
            if slot is not None:
                landing(slot, c).wait_recv()
                total += landed[slot, c]
            out_ref[:, columns(k, c)] = total * weight
        each(body)

    def blank(k):
        def body(c):
            out_ref[:, columns(k, c)] = jnp.zeros((rows, width), jnp.float32)
        each(body)

    no_up = jnp.logical_not(has_up)

    @pl.when(aux == 0)
    def _():
        finish(0, DIAG, None)
        pl.when(par == 0)(lambda: finish(1, INNER, 0))
        pl.when((par == 1) & has_up)(lambda: finish(1, 4, 0))
        pl.when((par == 1) & no_up)(lambda: blank(1))

    @pl.when(aux == 1)
    def _():
        pl.when(has_up)(lambda: finish(0, 2, 1))
        pl.when(no_up)(lambda: blank(0))
        pl.when((par == 0) & has_up)(lambda: finish(1, 4, 0))
        pl.when((par == 0) & no_up)(lambda: blank(1))

        @pl.when((par == 1) & two_up)
        def _():
            weight = mask_ref[0, 3].astype(jnp.float32)

            def body(c):
                landing(0, c).wait_recv()
                out_ref[:, columns(1, c)] = landed[0, c] * weight
            each(body)

        pl.when((par == 1) & jnp.logical_not(two_up))(lambda: blank(1))

    def drain(c):
        x_copy(c).wait_send()

        @pl.when(has_down)
        def _():
            down_own(c).wait_send()
            down_relay(c).wait_send()

        pl.when(two_up)(lambda: up_relay(c).wait_send())

        @pl.when(aux == 1)
        def _():
            sib_copy(DIAG, c).wait_send()
            sib_copy(INNER, c).wait_send()

        pl.when((aux == 0) & (par == 1))(lambda: forward(INNER, c, 0, neighbour).wait_send())

        @pl.when(has_up)
        def _():
            for phase in (0, 1):
                own, far = 2 + 2 * phase, 3 + 2 * phase
                own_holder = 1 - par * phase
                far_holder = par + phase - par * phase
                pl.when(aux != own_holder)(lambda: sib_copy(own, c).wait_send())
                pl.when(aux != far_holder)(lambda: sib_copy(far, c).wait_send())
                pl.when(aux == far_holder)(lambda: forward(far, c, phase, neighbour).wait_send())

            @pl.when(has_down)
            def _():
                pl.when(aux == 0)(lambda: sib_copy(UPPER, c).wait_send())
                pl.when(aux == 1)(lambda: forward(UPPER, c, 0, lower_odd).wait_send())

    each(drain)


def per_device(half, pair_mask):
    devices = lax.axis_size("orb")
    aux_count, blk, occ = half.shape
    depth, wide = aux_count // 2, blk // CHUNKS
    f32, bf16 = jnp.float32, jnp.bfloat16
    dma = pltpu.SemaphoreType.DMA
    return pl.pallas_call(
        functools.partial(kernel, devices),
        out_shape=jax.ShapeDtypeStruct((blk, 2 * blk), f32),
        in_specs=[pl.BlockSpec(memory_space=pl.ANY), pl.BlockSpec(memory_space=pltpu.SMEM)],
        out_specs=pl.BlockSpec(memory_space=pltpu.VMEM),
        scratch_shapes=[
            pltpu.VMEM((2, depth, blk, occ), bf16),
            pltpu.VMEM((depth, blk, occ), bf16),
            pltpu.VMEM((2, depth, blk, occ), bf16),
            pltpu.VMEM((depth, blk, occ), bf16),
            pltpu.VMEM((7, CHUNKS, blk, wide), f32),
            pltpu.VMEM((7, CHUNKS, blk, wide), f32),
            pltpu.VMEM((3, CHUNKS, blk, wide), f32),
            dma((2,)),
            dma((CHUNKS,)), dma((CHUNKS,)),
            dma((2, CHUNKS)), dma((2, CHUNKS)),
            dma((CHUNKS,)), dma((CHUNKS,)),
            dma((7, CHUNKS)), dma((7, CHUNKS)),
            dma((7, CHUNKS)), dma((3, CHUNKS)),
        ],
        compiler_params=pltpu.CompilerParams(
            collective_id=0, has_side_effects=True, vmem_limit_bytes=63 * 1024 * 1024
        ),
    )(half, pair_mask)


def solution(mesh):
    in_specs = (P("aux", ("grp", "orb"), None), P(("grp", "orb"), None))
    out_specs = P(("grp", "orb"), "aux")
    return jax.shard_map(
        per_device, mesh=mesh, in_specs=in_specs, out_specs=out_specs, check_vma=False
    )
```

```python
import functools

import jax
import jax.numpy as jnp
from jax import lax
from jax.experimental import pallas as pl
from jax.experimental.pallas import tpu as pltpu
from jax.sharding import PartitionSpec as P

MESH = pl.DeviceIdType.MESH
CHUNKS = 4
EARLY = 2
SPLIT = CHUNKS // 2
DIAG, INNER, UPPER = 0, 1, 6


def dot_nt(left, right):
    return lax.dot_general(left, right, (((1,), (1,)), ((), ())), preferred_element_type=jnp.float32)


def kernel(
    devices, half_ref, mask_ref, result, out_ref, pair, rest, above, below, part, sib, landed,
    load_sem, x_send, x_recv, down_send, down_recv, up_send, up_recv,
    sib_send, sib_recv, fwd_send, land_recv, out_send,
):
    pairs = devices // 2
    me = lax.axis_index("orb")
    aux = lax.axis_index("aux")
    p, par = lax.div(me, 2), lax.rem(me, 2)
    has_down, has_up, two_up = p > 0, p < pairs - 1, p < pairs - 2
    neighbour = {"orb": me + 1 - 2 * par}
    lower, upper, sibling = {"orb": me - 2}, {"orb": me + 2}, {"aux": 1 - aux}
    lower_odd = {"orb": me - 1 - par}
    depth = pair.shape[1]
    rows = pair.shape[2]
    width = rows // CHUNKS
    mine, other = depth * par, depth * (1 - par)

    def span(c):
        return pl.ds(pl.multiple_of(c * width, width), width)

    def remote(src, dst, send, recv, device):
        return pltpu.make_async_remote_copy(
            src_ref=src, dst_ref=dst, send_sem=send, recv_sem=recv, device_id=device, device_id_type=MESH
        )

    def x_copy(c):
        return remote(half_ref.at[pl.ds(other, depth), span(c), :], pair.at[par, :, span(c), :], x_send.at[c], x_recv.at[c], neighbour)

    def x_arrival(c):
        spot = pair.at[1 - par, :, span(c), :]
        return remote(spot, spot, x_send.at[c], x_recv.at[c], neighbour)

    def down_own(c):
        return remote(half_ref.at[pl.ds(mine, depth), span(c), :], above.at[par, :, span(c), :], down_send.at[0, c], down_recv.at[0, c], lower)

    def down_relay(c):
        return remote(pair.at[1 - par, :, span(c), :], above.at[1 - par, :, span(c), :], down_send.at[1, c], down_recv.at[1, c], lower)

    def down_arrival(phase, q, c):
        spot = above.at[q, :, span(c), :]
        return remote(spot, spot, down_send.at[phase, c], down_recv.at[phase, c], lower)

    def up_own(c):
        return remote(half_ref.at[pl.ds(mine, depth), span(c), :], below.at[:, span(c), :], up_send.at[c], up_recv.at[c], upper)

    def up_relay(c):
        return remote(pair.at[1, :, span(c), :], below.at[:, span(c), :], up_send.at[c], up_recv.at[c], upper)

    def sib_copy(s, c):
        return remote(part.at[s, c], sib.at[s, c], sib_send.at[s, c], sib_recv.at[s, c], sibling)

    def forward(s, c, slot, device):
        return remote(part.at[s, c], landed.at[slot, c], fwd_send.at[s, c], land_recv.at[slot, c], device)

    def each(body):
        def step(c, carry):
            body(c)
            return carry
        lax.fori_loop(0, CHUNKS, step, 0)

    barrier = pltpu.get_barrier_semaphore()

    def greet(device):
        pl.semaphore_signal(barrier, inc=1, device_id=device, device_id_type=MESH)

    greet(neighbour)
    greet(sibling)
    pl.when(has_down)(lambda: greet(lower))
    pl.when(has_up)(lambda: greet(upper))
    pl.when(has_down & (par == 0))(lambda: greet({"orb": me - 1}))
    pl.when(has_up & (par == 1))(lambda: greet({"orb": me + 1}))
    peers_down, peers_up = jnp.where(has_down, 1, 0), jnp.where(has_up, 1, 0)
    pl.semaphore_wait(barrier, 2 + peers_down * (2 - par) + peers_up * (1 + par))

    early = CHUNKS - par * (CHUNKS - EARLY)

    def launch(c):
        x_copy(c).start()
        pl.when(has_down & (c < early))(lambda: down_own(c).start())
        pl.when(two_up & (par == 1))(lambda: up_own(c).start())

    each(launch)
    load_mine = pltpu.make_async_copy(half_ref.at[pl.ds(mine, depth)], pair.at[par], load_sem.at[0])
    load_rest = pltpu.make_async_copy(half_ref.at[pl.ds(other, depth)], rest, load_sem.at[1])
    load_mine.start()
    load_rest.start()
    load_mine.wait()
    load_rest.wait()

    def diagonal(c):
        total = dot_nt(pair[par, 0], pair[par, 0, span(c), :])
        for i in range(1, depth):
            total += dot_nt(pair[par, i], pair[par, i, span(c), :])
        for i in range(depth):
            total += dot_nt(rest[i], rest[i, span(c), :])
        part[DIAG, c] = total
        pl.when(aux == 1)(lambda: sib_copy(DIAG, c).start())

    each(diagonal)

    def relay(c):
        x_arrival(c).wait_recv()
        pl.when(has_down)(lambda: down_relay(c).start())
        pl.when(two_up & (par == 0))(lambda: up_relay(c).start())

    each(relay)

    @pl.when(has_down & (par == 1))
    def _():
        for c in range(EARLY, CHUNKS):
            down_own(c).start()

    def diagonal_sum(c):
        sib_copy(DIAG, c).wait_recv()
        part[DIAG, c] += sib[DIAG, c]


    def product(left, right, c):
        total = dot_nt(left[0], right[0, span(c), :])
        for i in range(1, depth):
            total += dot_nt(left[i], right[i, span(c), :])
        return total

    def inner(c):
        part[INNER, c] = product(pair.at[0], pair.at[1], c)

        @pl.when(aux == 1)
        def _():
            sib_copy(INNER, c).start()

    each(inner)

    def inner_sum(c):
        sib_copy(INNER, c).wait_recv()
        part[INNER, c] += sib[INNER, c]
        pl.when(par == 1)(lambda: forward(INNER, c, 0, neighbour).start())

    @pl.when(aux == 0)
    def _():
        each(inner_sum)
        each(diagonal_sum)

    def landing(slot, c):
        spot = landed.at[slot, c]
        return remote(spot, spot, fwd_send.at[0, c], land_recv.at[slot, c], neighbour)

    def below_arrived(c):
        spot = below.at[:, span(c), :]
        remote(spot, spot, up_send.at[c], up_recv.at[c], upper).wait_recv()

    @pl.when(has_up)
    def _():
        def step(t, carry):
            middle = (t >= EARLY) & (t < EARLY + CHUNKS)
            q = jnp.where(par == 0, lax.div(t, CHUNKS), jnp.where(middle, 0, 1))
            c = jnp.where(par == 0, lax.rem(t, CHUNKS), jnp.where(middle, t - EARLY, jnp.where(t < EARLY, t, t - CHUNKS)))
            phase = par + q - 2 * par * q
            own, far = 2 + 2 * phase, 3 + 2 * phase
            own_holder = 1 - par * phase
            far_holder = par + phase - par * phase
            upper_tile = (q == 0) & has_down
            down_arrival(phase, q, c).wait_recv()
            part[far, c] = product(pair.at[1 - par], above.at[q], c)
            pl.when(aux != far_holder)(lambda: sib_copy(far, c).start())

            pl.when(upper_tile & (c == 0))(lambda: each(below_arrived))

            @pl.when(upper_tile)
            def _():
                part[UPPER, c] = product(below, above.at[q], c)
                pl.when(aux == 0)(lambda: sib_copy(UPPER, c).start())

            part[own, c] = product(pair.at[par], above.at[q], c)
            pl.when(aux != own_holder)(lambda: sib_copy(own, c).start())

            @pl.when(aux == far_holder)
            def _():
                sib_copy(far, c).wait_recv()
                part[far, c] += sib[far, c]
                forward(far, c, phase, neighbour).start()

            @pl.when(upper_tile & (aux == 1))
            def _():
                sib_copy(UPPER, c).wait_recv()
                part[UPPER, c] += sib[UPPER, c]
                pl.when(lax.div(c, SPLIT) != par)(lambda: forward(UPPER, c, 2, neighbour).start())

            @pl.when((t == EARLY + CHUNKS - 1) & has_down & (aux == 1))
            def _():
                for i in range(SPLIT):
                    k = par * SPLIT + i
                    landing(2, k).wait_recv()
                    part[UPPER, k] += landed[2, k]
                    forward(UPPER, k, 0, lower_odd).start()

            @pl.when(aux == own_holder)
            def _():
                sib_copy(own, c).wait_recv()
                part[own, c] += sib[own, c]

            return carry

        lax.fori_loop(0, 2 * CHUNKS, step, 0)

    def columns(k, c):
        return pl.ds(pl.multiple_of(k * rows + c * width, width), width)

    def store(k, c):
        return pltpu.make_async_copy(out_ref.at[:, columns(k, c)], result.at[:, columns(k, c)], out_send.at[k, c])

    def finish(k, s, slot):
        weight = mask_ref[0, 2 * aux + k].astype(jnp.float32)

        def body(c):
            total = part[s, c]
            if slot is not None:
                landing(slot, c).wait_recv()
                total += landed[slot, c]
            out_ref[:, columns(k, c)] = total * weight
            store(k, c).start()
        each(body)

    def blank(k):
        def body(c):
            out_ref[:, columns(k, c)] = jnp.zeros((rows, width), jnp.float32)
            store(k, c).start()
        each(body)

    no_up = jnp.logical_not(has_up)

    @pl.when(aux == 0)
    def _():
        finish(0, DIAG, None)
        pl.when(par == 0)(lambda: finish(1, INNER, 0))
        pl.when((par == 1) & has_up)(lambda: finish(1, 4, 0))
        pl.when((par == 1) & no_up)(lambda: blank(1))

    @pl.when(aux == 1)
    def _():
        pl.when(has_up)(lambda: finish(0, 2, 1))
        pl.when(no_up)(lambda: blank(0))
        pl.when((par == 0) & has_up)(lambda: finish(1, 4, 0))
        pl.when((par == 0) & no_up)(lambda: blank(1))

        @pl.when((par == 1) & two_up)
        def _():
            weight = mask_ref[0, 3].astype(jnp.float32)

            def body(c):
                landing(0, c).wait_recv()
                out_ref[:, columns(1, c)] = landed[0, c] * weight
                store(1, c).start()
            each(body)

        pl.when((par == 1) & jnp.logical_not(two_up))(lambda: blank(1))

    def drain(c):
        store(0, c).wait()
        store(1, c).wait()
        x_copy(c).wait_send()

        @pl.when(has_down)
        def _():
            down_own(c).wait_send()
            down_relay(c).wait_send()

        pl.when(two_up)(lambda: up_relay(c).wait_send())

        @pl.when(aux == 1)
        def _():
            sib_copy(DIAG, c).wait_send()
            sib_copy(INNER, c).wait_send()

        pl.when((aux == 0) & (par == 1))(lambda: forward(INNER, c, 0, neighbour).wait_send())

        @pl.when(has_up)
        def _():
            for phase in (0, 1):
                own, far = 2 + 2 * phase, 3 + 2 * phase
                own_holder = 1 - par * phase
                far_holder = par + phase - par * phase
                pl.when(aux != own_holder)(lambda: sib_copy(own, c).wait_send())
                pl.when(aux != far_holder)(lambda: sib_copy(far, c).wait_send())
                pl.when(aux == far_holder)(lambda: forward(far, c, phase, neighbour).wait_send())

            @pl.when(has_down)
            def _():
                pl.when(aux == 0)(lambda: sib_copy(UPPER, c).wait_send())
                pl.when(aux == 1)(lambda: forward(UPPER, c, 0, lower_odd).wait_send())

    each(drain)


def per_device(half, pair_mask):
    devices = lax.axis_size("orb")
    aux_count, blk, occ = half.shape
    depth, wide = aux_count // 2, blk // CHUNKS
    f32, bf16 = jnp.float32, jnp.bfloat16
    dma = pltpu.SemaphoreType.DMA
    return pl.pallas_call(
        functools.partial(kernel, devices),
        out_shape=jax.ShapeDtypeStruct((blk, 2 * blk), f32),
        in_specs=[pl.BlockSpec(memory_space=pl.ANY), pl.BlockSpec(memory_space=pltpu.SMEM)],
        out_specs=pl.BlockSpec(memory_space=pl.ANY),
        scratch_shapes=[
            pltpu.VMEM((blk, 2 * blk), f32),
            pltpu.VMEM((2, depth, blk, occ), bf16),
            pltpu.VMEM((depth, blk, occ), bf16),
            pltpu.VMEM((2, depth, blk, occ), bf16),
            pltpu.VMEM((depth, blk, occ), bf16),
            pltpu.VMEM((7, CHUNKS, blk, wide), f32),
            pltpu.VMEM((7, CHUNKS, blk, wide), f32),
            pltpu.VMEM((3, CHUNKS, blk, wide), f32),
            dma((2,)),
            dma((CHUNKS,)), dma((CHUNKS,)),
            dma((2, CHUNKS)), dma((2, CHUNKS)),
            dma((CHUNKS,)), dma((CHUNKS,)),
            dma((7, CHUNKS)), dma((7, CHUNKS)),
            dma((7, CHUNKS)), dma((3, CHUNKS)), dma((2, CHUNKS)),
        ],
        compiler_params=pltpu.CompilerParams(
            collective_id=0, has_side_effects=True, vmem_limit_bytes=63 * 1024 * 1024
        ),
    )(half, pair_mask)


def solution(mesh):
    in_specs = (P("aux", ("grp", "orb"), None), P(("grp", "orb"), None))
    out_specs = P(("grp", "orb"), "aux")
    return jax.shard_map(
        per_device, mesh=mesh, in_specs=in_specs, out_specs=out_specs, check_vma=False
    )
```
